32 devices in a mesh: rows: 16 (over z, y, x), cols: 2 (over core).
Axes of the slice: x: 2, y: 2, z: 4, core: 2. Of those that a mesh axis runs over, the one named last changes fastest.
Arguments:
- friction: float32 [512, 8192], P('rows', 'cols'), may hold values from 0.00015625 to 0.015625
- sources: int32 [512, 8192], P('rows', 'cols'), may hold values from 0 to 1, as said below
Outputs:
- cost: float32 [512, 8192], P('rows', 'cols')
- overview_one: float32 [256, 4096], P('rows', 'cols')
- overview_two: float32 [128, 2048], P('rows', 'cols')
- change: float32 [1], replicated
The draws below stay inside these ranges and needn't reach their ends.
Inputs may be any that keep to these rules, and one draw needn't show every extreme that they name: `sources`: at least one cell of the raster is a source.
All inputs are finite; a program needn't handle non-finite values.
Results may differ from the reference program's by a relative error of at most 0.00002.
Values sent between devices are 32-bit elements; how exact they have to be, the bound alone decides.
No kernel may reach another device: no remote copies, remote signals or barrier semaphores. Data moves between devices by JAX's collectives and lax.ppermute only.
A program may use at most 128 MiB of HBM per device.

```python
import math
import jax
import jax.numpy as jnp
from jax import lax

R_DEV = 32
C_DEV = 4096
ITERS = 2
NR = 512
NC = 8192


def draw_sources(key, part):
    first = jax.random.fold_in(key, 11)
    second = jax.random.fold_in(key, 23)
    third = jax.random.fold_in(key, 37)
    scattered = jax.random.randint(first, (NR, NC), 0, 4 * R_DEV * C_DEV) == 0
    row_pick = jax.random.randint(second, (), 0, NR)
    col_pick = jax.random.randint(third, (), 0, NC)
    forced = (lax.broadcasted_iota(jnp.int32, (NR, NC), 0) == row_pick) & (lax.broadcasted_iota(jnp.int32, (NR, NC), 1) == col_pick)
    return (scattered | forced).astype(jnp.int32)


def levels(rng, extent, cuts, smallest, largest):
    level = 1.0
    for axis_at, blocks in cuts:
        heights = jax.random.uniform(jax.random.fold_in(jax.random.fold_in(rng, 6), axis_at), (blocks,), jnp.float32, smallest / len(cuts), largest / len(cuts))
        level = level * jnp.repeat(jnp.exp(heights), extent[axis_at] // blocks).reshape((-1,) + (1,) * (len(extent) - 1 - axis_at))
    return level


def setup_inputs(seed: int = 0) -> dict:
    keys = jax.random.split(jax.random.key(seed), 3)
    friction = jnp.clip(jnp.exp(math.log(0.015625) - 4.6051702 * jax.random.uniform(keys[0], (NR, NC), jnp.float32) ** levels(keys[0], (NR, NC), ((0, 16), (1, 2)), -0.2, 0.2)), 0.00015625, 0.015625)
    sources = draw_sources(jax.random.fold_in(keys[2], 71), 0)
    return {"friction": friction, "sources": sources}


HUGE = 1e30


def link(earlier, later):
    return (jnp.minimum(later[0], earlier[0] + later[1]), earlier[1] + later[1])


def sweep(field, weights, axis, backward):
    return lax.associative_scan(link, (field, weights), reverse=backward, axis=axis)[0]


def pooled(image):
    height, width = image.shape
    return jnp.min(image.reshape(height // 2, 2, width // 2, 2), axis=(1, 3))


def reference(friction, sources):
    rimmed = jnp.pad(friction, 1)
    centre = rimmed[1:-1, 1:-1]
    w_down = 0.5 * (rimmed[:-2, 1:-1] + centre)
    w_up = 0.5 * (rimmed[2:, 1:-1] + centre)
    w_right = 0.5 * (rimmed[1:-1, :-2] + centre)
    w_left = 0.5 * (rimmed[1:-1, 2:] + centre)
    field = jnp.where(sources == 1, jnp.zeros_like(friction), jnp.full_like(friction, HUGE))
    previous = field
    for step in range(ITERS):
        previous = field
        field = sweep(field, w_down, 0, False)
        field = sweep(field, w_up, 0, True)
        field = sweep(field, w_right, 1, False)
        field = sweep(field, w_left, 1, True)
    change = jnp.max(previous - field).reshape(1)
    overview_one = pooled(field)
    overview_two = pooled(overview_one)
    return field, overview_one, overview_two, change
```

```python
import functools

import jax
import jax.numpy as jnp
from jax import lax
from jax.experimental import pallas as pl
from jax.experimental.pallas import tpu as pltpu
from jax.sharding import PartitionSpec as P

ITERS = 2
HUGE = 1e30
LANES = 128
SUBS = 8

VMEM = pl.BlockSpec(memory_space=pltpu.VMEM)
ANY = pl.BlockSpec(memory_space=pl.ANY)
PARAMS = pltpu.CompilerParams(vmem_limit_bytes=48 * 1024 * 1024)


def f32(*shape):
    return jax.ShapeDtypeStruct(shape, jnp.float32)


def lane_roll(x, shift):
    return pltpu.roll(x, shift % LANES, 1)


def sub_roll(x, shift):
    return pltpu.roll(x, shift % SUBS, 0)


def sub_index():
    return lax.broadcasted_iota(jnp.int32, (SUBS, LANES), 0)


def lane_index():
    return lax.broadcasted_iota(jnp.int32, (SUBS, LANES), 1)


def where_dense(t, width):
    per = width // SUBS // LANES
    return t // per, pl.ds((t % per) * LANES, LANES)


def segment_pass(f, g):
    low = list(g)
    edge = [None] + [0.5 * (f[r - 1] + f[r]) for r in range(1, len(f))]
    for r in range(1, len(f)):
        low[r] = jnp.minimum(low[r], low[r - 1] + edge[r])
    for r in range(len(f) - 2, -1, -1):
        low[r] = jnp.minimum(low[r], low[r + 1] + edge[r + 1])
    return low


def column_exits(f, low, total, sub):
    down = low[-1] + 0.5 * f[-1]
    up = low[0] + 0.5 * f[0]
    span_d = jnp.where(sub >= 1, total, HUGE)
    span_u = jnp.where(sub < SUBS - 1, total, HUGE)
    reach = 1
    while reach < SUBS:
        down = jnp.minimum(down, sub_roll(down, reach) + span_d)
        up = jnp.minimum(up, sub_roll(up, -reach) + span_u)
        if reach * 2 < SUBS:
            span_d = span_d + sub_roll(span_d, reach)
            span_u = span_u + sub_roll(span_u, -reach)
        reach *= 2
    enter_d = jnp.where(sub >= 1, sub_roll(down, 1), HUGE)
    enter_u = jnp.where(sub < SUBS - 1, sub_roll(up, -1), HUGE)
    return down, up, enter_d, enter_u


def prefix_totals(total, sub):
    before = total
    after = total
    reach = 1
    while reach < SUBS:
        before = before + jnp.where(sub >= reach, sub_roll(before, reach), 0.0)
        after = after + jnp.where(sub < SUBS - reach, sub_roll(after, -reach), 0.0)
        reach *= 2
    full = after[0:1, :]
    before = jnp.where(sub >= 1, sub_roll(before, 1), 0.0)
    after = jnp.where(sub < SUBS - 1, sub_roll(after, -1), 0.0)
    return before, after, full


def first_kernel(f_hbm, s_hbm, f_ref, low_ref, seg_ref, base_ref, pay_ref, f_buf, s_buf, exits, sems):
    tiles, height = f_buf.shape[0], f_buf.shape[1]
    width = tiles * LANES
    seg = height // SUBS
    place = lax.axis_index("rows")
    copies = []
    for t in range(tiles):
        cols = pl.ds(t * LANES, LANES)
        copies.append(pltpu.make_async_copy(f_hbm.at[:, cols], f_buf.at[t], sems.at[0, t]))
        copies.append(pltpu.make_async_copy(s_hbm.at[:, cols], s_buf.at[t], sems.at[1, t]))
    for copy in copies:
        copy.start()
    sub = sub_index()
    for t in range(tiles):
        copies[2 * t].wait()
        copies[2 * t + 1].wait()
        f = [f_buf[t, pl.ds(r, SUBS, stride=seg), :] for r in range(seg)]
        g = [
            jnp.where(s_buf[t, pl.ds(r, SUBS, stride=seg), :] == 1, 0.0, HUGE)
            for r in range(seg)
        ]
        low = segment_pass(f, g)
        total = functools.reduce(lambda a, b: a + b, f)
        down, up, enter_d, enter_u = column_exits(f, low, total, sub)
        before, after, full = prefix_totals(total, sub)
        for r in range(seg):
            f_ref[r, t] = f[r]
            low_ref[r, t] = low[r]
        seg_ref[0, t] = enter_d
        seg_ref[1, t] = enter_u
        base_ref[0, t] = before
        base_ref[1, t] = after
        a, b = where_dense(t, width)
        exits[0, pl.ds(a, 1), b] = down[SUBS - 1 : SUBS, :]
        exits[1, pl.ds(a, 1), b] = up[0:1, :]
        exits[2, pl.ds(a, 1), b] = full
    down, up, full = exits[0], exits[1], exits[2]
    for e in range(pay_ref.shape[0]):
        pay_ref[e, 0:SUBS, :] = jnp.where(e > place, down, up)
        pay_ref[e, SUBS : 2 * SUBS, :] = full


def lane_setup_kernel(f_ref, span_ref, right_ref, left_ref, total_ref):
    seg, tiles = f_ref.shape[0], f_ref.shape[1]
    levels = span_ref.shape[0]
    lane = lane_index()
    chunk = 8

    def step(i, unused):
        for r in range(seg):
            for q in range(chunk):
                t = i * chunk + q
                f = f_ref[r, t]
                half = 0.5 * f
                span = jnp.where(lane >= 1, lane_roll(half, 1) + half, HUGE)
                before = f
                after = f
                for k in range(levels):
                    span_ref[k, r, t] = span
                    reach = 1 << k
                    before = before + jnp.where(lane >= reach, lane_roll(before, reach), 0.0)
                    after = after + jnp.where(lane < LANES - reach, lane_roll(after, -reach), 0.0)
                    if k + 1 < levels:
                        span = span + lane_roll(span, reach)
                right_ref[r, t] = jnp.where(lane >= 1, lane_roll(before, 1), 0.0) + half
                left_ref[r, t] = jnp.where(lane < LANES - 1, lane_roll(after, -1), 0.0) + half
                total_ref[r, t] = jnp.broadcast_to(after[:, 0:1], (SUBS, LANES))
        return 0

    lax.fori_loop(0, tiles // chunk, step, 0)


def across_kernel(got_ref, full_ref, f_ref, low_ref, seg_ref, base_ref, span_ref, total_ref,
                  out_ref, exit_r_ref, exit_l_ref, pay_ref, enter, full_at):
    seg, tiles = f_ref.shape[0], f_ref.shape[1]
    width = tiles * LANES
    levels = span_ref.shape[0]
    peers = got_ref.shape[0]
    place = lax.axis_index("rows")

    def go_down(m, run):
        return jnp.minimum(got_ref[m, 0:SUBS, :], run + full_ref[m, full_at : full_at + SUBS, :])

    def go_up(i, run):
        m = peers - 1 - i
        return jnp.minimum(got_ref[m, 0:SUBS, :], run + full_ref[m, full_at : full_at + SUBS, :])

    nothing = jnp.full((SUBS, width // SUBS), HUGE, jnp.float32)
    enter[0] = lax.fori_loop(0, place, go_down, nothing)
    enter[1] = lax.fori_loop(0, peers - 1 - place, go_up, nothing)
    lane = lane_index()
    for t in range(tiles):
        a, b = where_dense(t, width)
        e_down = jnp.broadcast_to(enter[0, pl.ds(a, 1), b], (SUBS, LANES))
        e_up = jnp.broadcast_to(enter[1, pl.ds(a, 1), b], (SUBS, LANES))
        top = jnp.minimum(seg_ref[0, t], e_down + base_ref[0, t])
        bottom = jnp.minimum(seg_ref[1, t], e_up + base_ref[1, t])
        f = [f_ref[r, t] for r in range(seg)]
        half = [0.5 * x for x in f]
        c = [low_ref[r, t] for r in range(seg)]
        for r in range(seg):
            c[r] = jnp.minimum(c[r], top + half[r])
            top = top + f[r]
        for r in range(seg - 1, -1, -1):
            c[r] = jnp.minimum(c[r], bottom + half[r])
            bottom = bottom + f[r]
            out_ref[r, t] = c[r]
    chunk = 8

    def sweep(i, unused):
        c = [[out_ref[r, i * chunk + q] for q in range(chunk)] for r in range(seg)]
        for k in range(levels):
            reach = 1 << k
            for r in range(seg):
                for q in range(chunk):
                    span = span_ref[k, r, i * chunk + q]
                    x = c[r][q]
                    ahead = lane_roll(x, reach) + span
                    back = lane_roll(x + span, -reach)
                    c[r][q] = jnp.minimum(x, jnp.minimum(ahead, back))
        for r in range(seg):
            for q in range(chunk):
                t = i * chunk + q
                x = c[r][q]
                out_ref[r, t] = x
                y = x + 0.5 * f_ref[r, t]
                exit_r_ref[r, t] = jnp.broadcast_to(y[:, LANES - 1 : LANES], (SUBS, LANES))
                exit_l_ref[r, t] = jnp.broadcast_to(y[:, 0:1], (SUBS, LANES))
        return 0

    lax.fori_loop(0, tiles // chunk, sweep, 0)

    def chain(t, state):
        u = tiles - 1 - t
        rights = [jnp.minimum(exit_r_ref[r, t], state[0][r] + total_ref[r, t]) for r in range(seg)]
        lefts = [jnp.minimum(exit_l_ref[r, u], state[1][r] + total_ref[r, u]) for r in range(seg)]
        return rights, lefts

    none = [jnp.full((SUBS, LANES), HUGE, jnp.float32)] * seg
    rights, lefts = lax.fori_loop(0, tiles, chain, (none, none), unroll=4)
    pay = jnp.zeros((SUBS, LANES), jnp.float32)
    for r in range(seg):
        pay = jnp.where(lane == r, rights[r], pay)
        pay = jnp.where(lane == seg + r, lefts[r], pay)
    pay_ref[...] = pay


def enter_rows(pay, total_ref, exit_r_ref, exit_l_ref, enter_r, enter_l):
    seg, tiles = total_ref.shape[0], total_ref.shape[1]
    side = lax.axis_index("cols")
    rights = []
    lefts = []
    for r in range(seg):
        from_left = jnp.broadcast_to(pay[:, r : r + 1], (SUBS, LANES))
        from_right = jnp.broadcast_to(pay[:, seg + r : seg + r + 1], (SUBS, LANES))
        rights.append(jnp.where(side > 0, from_left, HUGE))
        lefts.append(jnp.where(side > 0, HUGE, from_right))

    def chain(t, state):
        u = tiles - 1 - t
        rights = []
        lefts = []
        for r in range(seg):
            enter_r[r, t] = state[0][r]
            enter_l[r, u] = state[1][r]
            rights.append(jnp.minimum(exit_r_ref[r, t], state[0][r] + total_ref[r, t]))
            lefts.append(jnp.minimum(exit_l_ref[r, u], state[1][r] + total_ref[r, u]))
        return rights, lefts

    lax.fori_loop(0, tiles, chain, (rights, lefts), unroll=4)


def down_kernel(got_ref, row_ref, exit_r_ref, exit_l_ref, right_ref, left_ref, total_ref, f_ref,
                prev_ref, low_ref, seg_ref, pay_ref, enter_r, enter_l, exits):
    seg, tiles = f_ref.shape[0], f_ref.shape[1]
    width = tiles * LANES
    place = lax.axis_index("rows")
    enter_rows(got_ref[...], total_ref, exit_r_ref, exit_l_ref, enter_r, enter_l)
    sub = sub_index()
    for t in range(tiles):
        f = [f_ref[r, t] for r in range(seg)]
        c = []
        for r in range(seg):
            across = jnp.minimum(enter_r[r, t] + right_ref[r, t], enter_l[r, t] + left_ref[r, t])
            c.append(jnp.minimum(row_ref[r, t], across))
            prev_ref[r, t] = c[r]
        low = segment_pass(f, c)
        total = functools.reduce(lambda a, b: a + b, f)
        down, up, enter_d, enter_u = column_exits(f, low, total, sub)
        for r in range(seg):
            low_ref[r, t] = low[r]
        seg_ref[0, t] = enter_d
        seg_ref[1, t] = enter_u
        a, b = where_dense(t, width)
        exits[0, pl.ds(a, 1), b] = down[SUBS - 1 : SUBS, :]
        exits[1, pl.ds(a, 1), b] = up[0:1, :]
    down, up = exits[0], exits[1]
    for e in range(pay_ref.shape[0]):
        pay_ref[e] = jnp.where(e > place, down, up)


def pick_even(x, y, lane):
    index = (2 * lane) % LANES
    x = jnp.take_along_axis(x, index, axis=1)
    y = jnp.take_along_axis(y, index, axis=1)
    return jnp.where(lane < LANES // 2, x, y)


def last_kernel(got_ref, row_ref, exit_r_ref, exit_l_ref, right_ref, left_ref, total_ref, prev_ref,
                cost_hbm, one_hbm, two_ref, pay_ref, enter_r, enter_l, cost_buf, one_buf, sems, sems_one):
    seg, tiles = total_ref.shape[0], total_ref.shape[1]
    enter_rows(got_ref[...], total_ref, exit_r_ref, exit_l_ref, enter_r, enter_l)
    lane = lane_index()
    worst = jnp.zeros((SUBS, LANES), jnp.float32)
    copies = []
    pooled = []
    wide = []
    for t in range(tiles):
        c = []
        for r in range(seg):
            across = jnp.minimum(enter_r[r, t] + right_ref[r, t], enter_l[r, t] + left_ref[r, t])
            c.append(jnp.minimum(row_ref[r, t], across))
            worst = jnp.maximum(worst, prev_ref[r, t] - c[r])
            cost_buf[t, pl.ds(r, SUBS, stride=seg), :] = c[r]
        cols = pl.ds(t * LANES, LANES)
        copies.append(pltpu.make_async_copy(cost_buf.at[t], cost_hbm.at[:, cols], sems.at[t]))
        copies[-1].start()
        pairs = [jnp.minimum(c[r], c[r + 1]) for r in range(0, seg, 2)]
        pooled.append([jnp.minimum(x, lane_roll(x, -1)) for x in pairs])
        if t % 2 == 1:
            u = t // 2
            ones = [pick_even(pooled[t - 1][r], pooled[t][r], lane) for r in range(seg // 2)]
            for r in range(seg // 2):
                one_buf[u, pl.ds(r, SUBS, stride=seg // 2), :] = ones[r]
            cols = pl.ds(u * LANES, LANES)
            copies.append(pltpu.make_async_copy(one_buf.at[u], one_hbm.at[:, cols], sems_one.at[u]))
            copies[-1].start()
            quads = [jnp.minimum(ones[r], ones[r + 1]) for r in range(0, seg // 2, 2)]
            wide.append([jnp.minimum(x, lane_roll(x, -1)) for x in quads])
        if t % 4 == 3:
            v = t // 4
            for r in range(seg // 4):
                two = pick_even(wide[2 * v][r], wide[2 * v + 1][r], lane)
                two_ref[:, v * LANES : (v + 1) * LANES] = two
    worst = jnp.max(worst, axis=0, keepdims=True)
    for e in range(pay_ref.shape[0]):
        pay_ref[e] = worst
    for copy in copies:
        copy.wait()


def change_kernel(got_ref, out_ref):
    worst = jnp.max(got_ref[...], axis=0)
    worst = jnp.max(worst, axis=1, keepdims=True)
    out_ref[...] = jnp.broadcast_to(worst, out_ref.shape)


def scratch(*shape, dtype=jnp.float32):
    return pltpu.VMEM(shape, dtype)


def shards(friction, sources):
    height, width = friction.shape
    tiles, seg, levels = width // LANES, height // SUBS, LANES.bit_length() - 1
    peers, sides = lax.axis_size("rows"), lax.axis_size("cols")
    short = width // SUBS
    block = f32(seg, tiles, SUBS, LANES)
    pair = f32(2, tiles, SUBS, LANES)
    held = [scratch(seg, tiles, SUBS, LANES)] * 2
    swap = [(i, sides - 1 - i) for i in range(sides)]

    f, low, enters, base, pay = pl.pallas_call(
        first_kernel,
        out_shape=(block, block, pair, pair, f32(peers, 2 * SUBS, short)),
        in_specs=[ANY, ANY],
        out_specs=[VMEM] * 5,
        scratch_shapes=[
            scratch(tiles, height, LANES),
            scratch(tiles, height, LANES, dtype=jnp.int32),
            scratch(3, SUBS, short),
            pltpu.SemaphoreType.DMA((2, tiles)),
        ],
        compiler_params=PARAMS,
        name="first",
    )(friction, sources)
    first_got = lax.all_to_all(pay, "rows", 0, 0)
    spans, rights, lefts, totals = pl.pallas_call(
        lane_setup_kernel,
        out_shape=(f32(levels, seg, tiles, SUBS, LANES), block, block, block),
        in_specs=[VMEM],
        out_specs=[VMEM] * 4,
        compiler_params=PARAMS,
        name="lane_setup",
    )(f)

    def across(got, low, enters):
        return pl.pallas_call(
            functools.partial(across_call, SUBS),
            out_shape=(block, block, block, f32(SUBS, LANES)),
            in_specs=[VMEM] * 8,
            out_specs=[VMEM] * 4,
            scratch_shapes=[scratch(2, SUBS, short)],
            compiler_params=PARAMS,
            name="across",
        )(got, first_got, f, low, enters, base, spans, totals)

    row, exit_r, exit_l, side_pay = across(first_got, low, enters)
    side_got = lax.ppermute(side_pay, "cols", swap)
    prev, low, enters, pay = pl.pallas_call(
        down_kernel,
        out_shape=(block, block, pair, f32(peers, SUBS, short)),
        in_specs=[VMEM] * 8,
        out_specs=[VMEM] * 4,
        scratch_shapes=held + [scratch(2, SUBS, short)],
        compiler_params=PARAMS,
        name="down",
    )(side_got, row, exit_r, exit_l, rights, lefts, totals, f)
    got = lax.all_to_all(pay, "rows", 0, 0)
    row, exit_r, exit_l, side_pay = across(got, low, enters)
    side_got = lax.ppermute(side_pay, "cols", swap)
    cost, one, two, pay = pl.pallas_call(
        last_kernel,
        out_shape=(
            f32(height, width),
            f32(height // 2, width // 2),
            f32(height // 4, width // 4),
            f32(peers * sides, 1, LANES),
        ),
        in_specs=[VMEM] * 8,
        out_specs=[ANY, ANY, VMEM, VMEM],
        scratch_shapes=held
        + [
            scratch(tiles, height, LANES),
            scratch(tiles // 2, height // 2, LANES),
            pltpu.SemaphoreType.DMA((tiles,)),
            pltpu.SemaphoreType.DMA((tiles // 2,)),
        ],
        compiler_params=PARAMS,
        name="last",
    )(side_got, row, exit_r, exit_l, rights, lefts, totals, prev)
    got = lax.all_to_all(pay, ("rows", "cols"), 0, 0)
    change = pl.pallas_call(
        change_kernel,
        out_shape=f32(1, LANES),
        in_specs=[VMEM],
        out_specs=VMEM,
        compiler_params=PARAMS,
        name="change",
    )(got)
    return cost, one, two, change[0, :1]


def across_call(full_at, *refs):
    across_kernel(*refs, full_at=full_at)


def solution(mesh):
    placed = (P("rows", "cols"), P("rows", "cols"))
    return jax.shard_map(
        shards,
        mesh=mesh,
        in_specs=placed,
        out_specs=(P("rows", "cols"), P("rows", "cols"), P("rows", "cols"), P()),
        check_vma=False,
    )
```

```python
import functools

import jax
import jax.numpy as jnp
from jax import lax
from jax.experimental import pallas as pl
from jax.experimental.pallas import tpu as pltpu
from jax.sharding import PartitionSpec as P

ITERS = 2
HUGE = 1e30
LANES = 128
SUBS = 8

VMEM = pl.BlockSpec(memory_space=pltpu.VMEM)
ANY = pl.BlockSpec(memory_space=pltpu.HBM)
PARAMS = pltpu.CompilerParams(vmem_limit_bytes=16 * 1024 * 1024)
FIRST_PARAMS = pltpu.CompilerParams(vmem_limit_bytes=52 * 1024 * 1024)


def f32(*shape):
    return jax.ShapeDtypeStruct(shape, jnp.float32)


def lane_roll(x, shift):
    return pltpu.roll(x, shift % LANES, 1)


def sub_roll(x, shift):
    return pltpu.roll(x, shift % SUBS, 0)


def sub_index():
    return lax.broadcasted_iota(jnp.int32, (SUBS, LANES), 0)


def lane_index():
    return lax.broadcasted_iota(jnp.int32, (SUBS, LANES), 1)


def where_dense(t, width):
    per = width // SUBS // LANES
    return t // per, pl.ds((t % per) * LANES, LANES)


def segment_pass(f, g):
    low = list(g)
    edge = [None] + [0.5 * (f[r - 1] + f[r]) for r in range(1, len(f))]
    for r in range(1, len(f)):
        low[r] = jnp.minimum(low[r], low[r - 1] + edge[r])
    for r in range(len(f) - 2, -1, -1):
        low[r] = jnp.minimum(low[r], low[r + 1] + edge[r + 1])
    return low


def column_exits(f, low, total, sub):
    down = low[-1] + 0.5 * f[-1]
    up = low[0] + 0.5 * f[0]
    span_d = jnp.where(sub >= 1, total, HUGE)
    span_u = jnp.where(sub < SUBS - 1, total, HUGE)
    reach = 1
    while reach < SUBS:
        down = jnp.minimum(down, sub_roll(down, reach) + span_d)
        up = jnp.minimum(up, sub_roll(up, -reach) + span_u)
        if reach * 2 < SUBS:
            span_d = span_d + sub_roll(span_d, reach)
            span_u = span_u + sub_roll(span_u, -reach)
        reach *= 2
    enter_d = jnp.where(sub >= 1, sub_roll(down, 1), HUGE)
    enter_u = jnp.where(sub < SUBS - 1, sub_roll(up, -1), HUGE)
    return down, up, enter_d, enter_u


def prefix_totals(total, sub):
    before = total
    after = total
    reach = 1
    while reach < SUBS:
        before = before + jnp.where(sub >= reach, sub_roll(before, reach), 0.0)
        after = after + jnp.where(sub < SUBS - reach, sub_roll(after, -reach), 0.0)
        reach *= 2
    full = after[0:1, :]
    before = jnp.where(sub >= 1, sub_roll(before, 1), 0.0)
    after = jnp.where(sub < SUBS - 1, sub_roll(after, -1), 0.0)
    return before, after, full


def first_kernel(f_hbm, s_hbm, f_ref, low_ref, seg_ref, base_ref, pay_ref, f_in, s_in, f_buf, s_buf, sems):
    tiles, height = f_buf.shape[0], f_buf.shape[1]
    width = tiles * LANES
    seg = height // SUBS
    chunks = sems.shape[1]
    part = tiles // chunks
    copies = []
    for i in range(chunks):
        cols = pl.ds(i * part * LANES, part * LANES)
        copies.append(pltpu.make_async_copy(f_hbm.at[:, cols], f_in.at[:, cols], sems.at[0, i]))
        copies.append(pltpu.make_async_copy(s_hbm.at[:, cols], s_in.at[:, cols], sems.at[1, i]))
    for copy in copies:
        copy.start()
    sub = sub_index()
    for t in range(tiles):
        if t % part == 0:
            copies[2 * (t // part)].wait()
            copies[2 * (t // part) + 1].wait()
        cols = pl.ds(t * LANES, LANES)
        f_buf[t] = f_in[:, cols]
        s_buf[t] = jnp.where(s_in[:, cols] == 1, 0.0, HUGE)
        f = [f_buf[t, pl.ds(r, SUBS, stride=seg), :] for r in range(seg)]
        g = [s_buf[t, pl.ds(r, SUBS, stride=seg), :] for r in range(seg)]
        low = segment_pass(f, g)
        total = functools.reduce(lambda a, b: a + b, f)
        down, up, enter_d, enter_u = column_exits(f, low, total, sub)
        before, after, full = prefix_totals(total, sub)
        for r in range(seg):
            f_ref[r, t] = f[r]
            low_ref[r, t] = low[r]
        seg_ref[0, t] = enter_d
        seg_ref[1, t] = enter_u
        base_ref[0, t] = before
        base_ref[1, t] = after
        a, b = where_dense(t, width)
        pay_ref[0, pl.ds(a, 1), b] = down[SUBS - 1 : SUBS, :]
        pay_ref[1, pl.ds(a, 1), b] = up[0:1, :]
        pay_ref[2, pl.ds(a, 1), b] = full


def join_kernel(stride, radix, xor, *refs):
    pays, refs = refs[:radix], refs[radix:]
    held, refs = (None, refs) if stride == 1 else (refs[0], refs[1:])
    state_ref, out_ref, tops = refs
    mine = (lax.axis_index("rows") // stride) % radix
    count = pays[0].shape[0] - 2
    for k in range(radix):
        m = mine ^ k if xor else (mine - k + radix) % radix
        tops[0, m] = pays[k][0]
        tops[1, m] = pays[k][1]
        total = pays[k][2]
        for i in range(1, count):
            total = total + pays[k][2 + i]
        tops[2, m] = total
        for i in range(count):
            out_ref[2 + m * count + i] = pays[k][2 + i]
    shape = tops.shape[2:]
    for way in range(2):
        enter = run = jnp.full(shape, HUGE, jnp.float32)
        base = jnp.zeros(shape, jnp.float32)
        for m in range(radix) if way == 0 else range(radix - 1, -1, -1):
            enter = jnp.where(mine == m, run, enter)
            run = jnp.minimum(tops[way, m], run + tops[2, m])
            passed = mine > m if way == 0 else mine < m
            base = base + jnp.where(passed, tops[2, m], 0.0)
        out_ref[way] = run
        if held is None:
            state_ref[way] = enter
            state_ref[2 + way] = base
        else:
            state_ref[way] = jnp.minimum(held[way], enter + held[2 + way])
            state_ref[2 + way] = base + held[2 + way]


def gather_kernel(got_ref, full_ref, enter_ref):
    peers = got_ref.shape[0]
    place = lax.axis_index("rows")

    def go_down(m, run):
        return jnp.minimum(got_ref[m], run + full_ref[2 + m])

    def go_up(i, run):
        m = peers - 1 - i
        return jnp.minimum(got_ref[m], run + full_ref[2 + m])

    nothing = jnp.full(got_ref.shape[1:], HUGE, jnp.float32)
    enter_ref[0] = lax.fori_loop(0, place, go_down, nothing)
    enter_ref[1] = lax.fori_loop(0, peers - 1 - place, go_up, nothing)


def lane_weights(kind, reach):
    source = lax.broadcasted_iota(jnp.int32, (LANES, LANES), 0)
    target = lax.broadcasted_iota(jnp.int32, (LANES, LANES), 1)
    if kind == "span":
        inner = (source > target - reach) & (source < target)
        ends = (source == target - reach) | (source == target)
    elif kind == "right":
        inner, ends = source < target, source == target
    elif kind == "left":
        inner, ends = source > target, source == target
    else:
        inner, ends = source >= 0, source < 0
    return jnp.where(inner, 1.0, jnp.where(ends, 0.5, 0.0))


def lane_kernel(kinds, f_ref, *refs):
    outs, weights = refs[:-1], refs[-1]
    seg, tiles = f_ref.shape[0], f_ref.shape[1]
    chunk = tiles
    for k, kind in enumerate(kinds):
        weights[k] = lane_weights(*kind)
    lane = lane_index()[None]

    def step(i, unused):
        r, at = i // (tiles // chunk), (i % (tiles // chunk)) * chunk
        f = f_ref[r, pl.ds(at, chunk)].reshape(chunk * SUBS, LANES)

        def mixed(k):
            y = jnp.dot(f, weights[k], precision=lax.Precision.HIGHEST, preferred_element_type=jnp.float32)
            return y.reshape(chunk, SUBS, LANES)

        for k, (kind, reach) in enumerate(kinds):
            if kind == "span":
                outs[0][k, r, pl.ds(at, chunk)] = jnp.where(lane >= reach, mixed(k), HUGE)
            else:
                outs[k][r, pl.ds(at, chunk)] = mixed(k)
        return 0

    lax.fori_loop(0, seg * (tiles // chunk), step, 0)


def across_kernel(enter, f_ref, low_ref, seg_ref, base_ref, span_ref, total_ref,
                  out_ref, exit_r_ref, exit_l_ref, pay_ref):
    seg, tiles = f_ref.shape[0], f_ref.shape[1]
    width = tiles * LANES
    levels = span_ref.shape[0]
    lane = lane_index()
    for t in range(tiles):
        a, b = where_dense(t, width)
        e_down = jnp.broadcast_to(enter[0, pl.ds(a, 1), b], (SUBS, LANES))
        e_up = jnp.broadcast_to(enter[1, pl.ds(a, 1), b], (SUBS, LANES))
        top = jnp.minimum(seg_ref[0, t], e_down + base_ref[0, t])
        bottom = jnp.minimum(seg_ref[1, t], e_up + base_ref[1, t])
        f = [f_ref[r, t] for r in range(seg)]
        half = [0.5 * x for x in f]
        c = [low_ref[r, t] for r in range(seg)]
        for r in range(seg):
            c[r] = jnp.minimum(c[r], top + half[r])
            top = top + f[r]
        for r in range(seg - 1, -1, -1):
            c[r] = jnp.minimum(c[r], bottom + half[r])
            bottom = bottom + f[r]
            out_ref[r, t] = c[r]
    chunk = 16

    def sweep(i, unused):
        c = [[out_ref[r, i * chunk + q] for q in range(chunk)] for r in range(seg)]
        for k in range(levels):
            reach = 1 << k
            for r in range(seg):
                for q in range(chunk):
                    span = span_ref[k, r, i * chunk + q]
                    x = c[r][q]
                    ahead = lane_roll(x, reach) + span
                    back = lane_roll(x + span, -reach)
                    c[r][q] = jnp.minimum(x, jnp.minimum(ahead, back))
        for r in range(seg):
            for q in range(chunk):
                t = i * chunk + q
                x = c[r][q]
                out_ref[r, t] = x
                y = x + 0.5 * f_ref[r, t]
                exit_r_ref[r, t] = jnp.broadcast_to(y[:, LANES - 1 : LANES], (SUBS, LANES))
                exit_l_ref[r, t] = jnp.broadcast_to(y[:, 0:1], (SUBS, LANES))
        return 0

    lax.fori_loop(0, tiles // chunk, sweep, 0)

    def chain(t, state):
        u = tiles - 1 - t
        rights = [jnp.minimum(exit_r_ref[r, t], state[0][r] + total_ref[r, t]) for r in range(seg)]
        lefts = [jnp.minimum(exit_l_ref[r, u], state[1][r] + total_ref[r, u]) for r in range(seg)]
        return rights, lefts

    none = [jnp.full((SUBS, LANES), HUGE, jnp.float32)] * seg
    rights, lefts = lax.fori_loop(0, tiles, chain, (none, none), unroll=4)
    pay = jnp.zeros((SUBS, LANES), jnp.float32)
    for r in range(seg):
        pay = jnp.where(lane == r, rights[r], pay)
        pay = jnp.where(lane == seg + r, lefts[r], pay)
    pay_ref[...] = pay


def enter_rows(pay, total_ref, exit_r_ref, exit_l_ref, enter_r, enter_l):
    seg, tiles = total_ref.shape[0], total_ref.shape[1]
    side = lax.axis_index("cols")
    rights = []
    lefts = []
    for r in range(seg):
        from_left = jnp.broadcast_to(pay[:, r : r + 1], (SUBS, LANES))
        from_right = jnp.broadcast_to(pay[:, seg + r : seg + r + 1], (SUBS, LANES))
        rights.append(jnp.where(side > 0, from_left, HUGE))
        lefts.append(jnp.where(side > 0, HUGE, from_right))

    def chain(t, state):
        u = tiles - 1 - t
        rights = []
        lefts = []
        for r in range(seg):
            enter_r[r, t] = state[0][r]
            enter_l[r, u] = state[1][r]
            rights.append(jnp.minimum(exit_r_ref[r, t], state[0][r] + total_ref[r, t]))
            lefts.append(jnp.minimum(exit_l_ref[r, u], state[1][r] + total_ref[r, u]))
        return rights, lefts

    lax.fori_loop(0, tiles, chain, (rights, lefts), unroll=4)


def down_kernel(got_ref, row_ref, exit_r_ref, exit_l_ref, right_ref, left_ref, total_ref, f_ref,
                prev_ref, low_ref, seg_ref, pay_ref, enter_r, enter_l, exits):
    seg, tiles = f_ref.shape[0], f_ref.shape[1]
    width = tiles * LANES
    place = lax.axis_index("rows")
    enter_rows(got_ref[...], total_ref, exit_r_ref, exit_l_ref, enter_r, enter_l)
    sub = sub_index()
    for t in range(tiles):
        f = [f_ref[r, t] for r in range(seg)]
        c = []
        for r in range(seg):
            across = jnp.minimum(enter_r[r, t] + right_ref[r, t], enter_l[r, t] + left_ref[r, t])
            c.append(jnp.minimum(row_ref[r, t], across))
            prev_ref[r, t] = c[r]
        low = segment_pass(f, c)
        total = functools.reduce(lambda a, b: a + b, f)
        down, up, enter_d, enter_u = column_exits(f, low, total, sub)
        for r in range(seg):
            low_ref[r, t] = low[r]
        seg_ref[0, t] = enter_d
        seg_ref[1, t] = enter_u
        a, b = where_dense(t, width)
        exits[0, pl.ds(a, 1), b] = down[SUBS - 1 : SUBS, :]
        exits[1, pl.ds(a, 1), b] = up[0:1, :]
    down, up = exits[0], exits[1]
    for e in range(pay_ref.shape[0]):
        pay_ref[e] = jnp.where(e > place, down, up)


def pick_even(x, y, lane):
    index = (2 * lane) % LANES
    x = jnp.take_along_axis(x, index, axis=1)
    y = jnp.take_along_axis(y, index, axis=1)
    return jnp.where(lane < LANES // 2, x, y)


def last_kernel(got_ref, row_ref, exit_r_ref, exit_l_ref, right_ref, left_ref, total_ref, prev_ref,
                cost_hbm, one_hbm, two_ref, pay_ref, enter_r, enter_l, cost_buf, one_buf, sems, sems_one):
    seg, tiles = total_ref.shape[0], total_ref.shape[1]
    enter_rows(got_ref[...], total_ref, exit_r_ref, exit_l_ref, enter_r, enter_l)
    lane = lane_index()
    worst = jnp.zeros((SUBS, LANES), jnp.float32)
    copies = []
    pooled = []
    wide = []
    for t in range(tiles):
        c = []
        for r in range(seg):
            across = jnp.minimum(enter_r[r, t] + right_ref[r, t], enter_l[r, t] + left_ref[r, t])
            c.append(jnp.minimum(row_ref[r, t], across))
            worst = jnp.maximum(worst, prev_ref[r, t] - c[r])
            cost_buf[t, pl.ds(r, SUBS, stride=seg), :] = c[r]
        cols = pl.ds(t * LANES, LANES)
        copies.append(pltpu.make_async_copy(cost_buf.at[t], cost_hbm.at[:, cols], sems.at[t]))
        copies[-1].start()
        pairs = [jnp.minimum(c[r], c[r + 1]) for r in range(0, seg, 2)]
        pooled.append([jnp.minimum(x, lane_roll(x, -1)) for x in pairs])
        if t % 2 == 1:
            u = t // 2
            ones = [pick_even(pooled[t - 1][r], pooled[t][r], lane) for r in range(seg // 2)]
            for r in range(seg // 2):
                one_buf[u, pl.ds(r, SUBS, stride=seg // 2), :] = ones[r]
            cols = pl.ds(u * LANES, LANES)
            copies.append(pltpu.make_async_copy(one_buf.at[u], one_hbm.at[:, cols], sems_one.at[u]))
            copies[-1].start()
            quads = [jnp.minimum(ones[r], ones[r + 1]) for r in range(0, seg // 2, 2)]
            wide.append([jnp.minimum(x, lane_roll(x, -1)) for x in quads])
        if t % 4 == 3:
            v = t // 4
            for r in range(seg // 4):
                two = pick_even(wide[2 * v][r], wide[2 * v + 1][r], lane)
                two_ref[:, v * LANES : (v + 1) * LANES] = two
    worst = jnp.max(worst, axis=0, keepdims=True)
    for e in range(pay_ref.shape[0]):
        pay_ref[e] = worst
    for copy in copies:
        copy.wait()


def change_kernel(got_ref, out_ref):
    worst = jnp.max(got_ref[...], axis=0)
    worst = jnp.max(worst, axis=1, keepdims=True)
    out_ref[...] = jnp.broadcast_to(worst, out_ref.shape)


def scratch(*shape, dtype=jnp.float32):
    return pltpu.VMEM(shape, dtype)


def digits(count):
    stride, rest, found = 1, count, []
    while rest > 1:
        radix = next((k for k in (4, 2) if rest % k == 0), rest)
        found.append((stride, radix))
        stride, rest = stride * radix, rest // radix
    return found


def partners(count, stride, radix, step):
    xor = radix & (radix - 1) == 0
    pairs = []
    for i in range(count):
        mine = (i // stride) % radix
        other = mine ^ step if xor else (mine + step) % radix
        pairs.append((i, i + (other - mine) * stride))
    return pairs


def shards(friction, sources):
    height, width = friction.shape
    tiles, seg, levels = width // LANES, height // SUBS, LANES.bit_length() - 1
    peers, sides = lax.axis_size("rows"), lax.axis_size("cols")
    short = width // SUBS
    block = f32(seg, tiles, SUBS, LANES)
    pair = f32(2, tiles, SUBS, LANES)
    held = [scratch(seg, tiles, SUBS, LANES)] * 2
    swap = [(i, sides - 1 - i) for i in range(sides)]
    chunks = 4

    f, low, enters, base, pay = pl.pallas_call(
        first_kernel,
        out_shape=(block, block, pair, pair, f32(3, SUBS, short)),
        in_specs=[ANY, ANY],
        out_specs=[VMEM] * 5,
        scratch_shapes=[
            scratch(height, width),
            scratch(height, width, dtype=jnp.int32),
            scratch(tiles, height, LANES),
            scratch(tiles, height, LANES),
            pltpu.SemaphoreType.DMA((2, chunks)),
        ],
        compiler_params=FIRST_PARAMS,
        name="first",
    )(friction, sources)

    def lane_call(kinds, outs, name):
        flops = 12 * len(kinds) * height * width * LANES
        return pl.pallas_call(
            functools.partial(lane_kernel, kinds),
            out_shape=outs,
            in_specs=[VMEM],
            out_specs=[VMEM] * len(outs),
            scratch_shapes=[scratch(len(kinds), LANES, LANES)],
            compiler_params=PARAMS,
            cost_estimate=pl.CostEstimate(flops=flops, bytes_accessed=4 * height * width, transcendentals=0),
            name=name,
        )(f)

    (spans,) = lane_call(
        [("span", 1 << k) for k in range(levels)], (f32(levels, seg, tiles, SUBS, LANES),), "lane_spans"
    )
    rights, lefts, totals = lane_call([("right", 0), ("left", 0), ("total", 0)], (block,) * 3, "lane_sums")

    state = ()
    for stride, radix in digits(peers):
        pays = [pay] + [
            lax.ppermute(pay, "rows", partners(peers, stride, radix, k)) for k in range(1, radix)
        ]
        state, pay = pl.pallas_call(
            functools.partial(join_kernel, stride, radix, radix & (radix - 1) == 0),
            out_shape=(f32(4, SUBS, short), f32(2 + stride * radix, SUBS, short)),
            in_specs=[VMEM] * (radix + (stride > 1)),
            out_specs=[VMEM] * 2,
            scratch_shapes=[scratch(3, radix, SUBS, short)],
            compiler_params=PARAMS,
            name="join",
        )(*pays, *([state] if stride > 1 else []))
    fulls = pay

    def across(enter, low, enters):
        return pl.pallas_call(
            across_kernel,
            out_shape=(block, block, block, f32(SUBS, LANES)),
            in_specs=[VMEM] * 7,
            out_specs=[VMEM] * 4,
            compiler_params=PARAMS,
            name="across",
        )(enter, f, low, enters, base, spans, totals)

    row, exit_r, exit_l, side_pay = across(state, low, enters)
    side_got = lax.ppermute(side_pay, "cols", swap)
    prev, low, enters, pay = pl.pallas_call(
        down_kernel,
        out_shape=(block, block, pair, f32(peers, SUBS, short)),
        in_specs=[VMEM] * 8,
        out_specs=[VMEM] * 4,
        scratch_shapes=held + [scratch(2, SUBS, short)],
        compiler_params=PARAMS,
        name="down",
    )(side_got, row, exit_r, exit_l, rights, lefts, totals, f)
    got = lax.all_to_all(pay, "rows", 0, 0)
    enter = pl.pallas_call(
        gather_kernel,
        out_shape=f32(2, SUBS, short),
        in_specs=[VMEM] * 2,
        out_specs=VMEM,
        compiler_params=PARAMS,
        name="gather",
    )(got, fulls)
    row, exit_r, exit_l, side_pay = across(enter, low, enters)
    side_got = lax.ppermute(side_pay, "cols", swap)
    cost, one, two, pay = pl.pallas_call(
        last_kernel,
        out_shape=(
            f32(height, width),
            f32(height // 2, width // 2),
            f32(height // 4, width // 4),
            f32(peers * sides, 1, LANES),
        ),
        in_specs=[VMEM] * 8,
        out_specs=[ANY, ANY, VMEM, VMEM],
        scratch_shapes=held
        + [
            scratch(tiles, height, LANES),
            scratch(tiles // 2, height // 2, LANES),
            pltpu.SemaphoreType.DMA((tiles,)),
            pltpu.SemaphoreType.DMA((tiles // 2,)),
        ],
        compiler_params=PARAMS,
        name="last",
    )(side_got, row, exit_r, exit_l, rights, lefts, totals, prev)
    got = lax.all_to_all(pay, ("rows", "cols"), 0, 0)
    change = pl.pallas_call(
        change_kernel,
        out_shape=f32(1, LANES),
        in_specs=[VMEM],
        out_specs=VMEM,
        compiler_params=PARAMS,
        name="change",
    )(got)
    return cost, one, two, change[0, :1]


def solution(mesh):
    placed = (P("rows", "cols"), P("rows", "cols"))
    return jax.shard_map(
        shards,
        mesh=mesh,
        in_specs=placed,
        out_specs=(P("rows", "cols"), P("rows", "cols"), P("rows", "cols"), P()),
        check_vma=False,
    )
```

```python
import functools

import jax
import jax.numpy as jnp
from jax import lax
from jax.experimental import pallas as pl
from jax.experimental.pallas import tpu as pltpu
from jax.sharding import PartitionSpec as P

ITERS = 2
HUGE = 1e30
LANES = 128
SUBS = 8

VMEM = pl.BlockSpec(memory_space=pltpu.VMEM)
ANY = pl.BlockSpec(memory_space=pltpu.HBM)
PARAMS = pltpu.CompilerParams(vmem_limit_bytes=16 * 1024 * 1024)
FIRST_PARAMS = pltpu.CompilerParams(vmem_limit_bytes=52 * 1024 * 1024)


def f32(*shape):
    return jax.ShapeDtypeStruct(shape, jnp.float32)


def lane_roll(x, shift):
    return pltpu.roll(x, shift % LANES, 1)


def sub_roll(x, shift):
    return pltpu.roll(x, shift % SUBS, 0)


def sub_index():
    return lax.broadcasted_iota(jnp.int32, (SUBS, LANES), 0)


def lane_index():
    return lax.broadcasted_iota(jnp.int32, (SUBS, LANES), 1)


def where_dense(t, width):
    per = width // SUBS // LANES
    return t // per, pl.ds((t % per) * LANES, LANES)


def segment_pass(f, g):
    low = list(g)
    edge = [None] + [0.5 * (f[r - 1] + f[r]) for r in range(1, len(f))]
    for r in range(1, len(f)):
        low[r] = jnp.minimum(low[r], low[r - 1] + edge[r])
    for r in range(len(f) - 2, -1, -1):
        low[r] = jnp.minimum(low[r], low[r + 1] + edge[r + 1])
    return low


def column_exits(f, low, total, sub):
    down = low[-1] + 0.5 * f[-1]
    up = low[0] + 0.5 * f[0]
    span_d = jnp.where(sub >= 1, total, HUGE)
    span_u = jnp.where(sub < SUBS - 1, total, HUGE)
    reach = 1
    while reach < SUBS:
        down = jnp.minimum(down, sub_roll(down, reach) + span_d)
        up = jnp.minimum(up, sub_roll(up, -reach) + span_u)
        if reach * 2 < SUBS:
            span_d = span_d + sub_roll(span_d, reach)
            span_u = span_u + sub_roll(span_u, -reach)
        reach *= 2
    enter_d = jnp.where(sub >= 1, sub_roll(down, 1), HUGE)
    enter_u = jnp.where(sub < SUBS - 1, sub_roll(up, -1), HUGE)
    return down, up, enter_d, enter_u


def prefix_totals(total, sub):
    before = total
    after = total
    reach = 1
    while reach < SUBS:
        before = before + jnp.where(sub >= reach, sub_roll(before, reach), 0.0)
        after = after + jnp.where(sub < SUBS - reach, sub_roll(after, -reach), 0.0)
        reach *= 2
    full = after[0:1, :]
    before = jnp.where(sub >= 1, sub_roll(before, 1), 0.0)
    after = jnp.where(sub < SUBS - 1, sub_roll(after, -1), 0.0)
    return before, after, full


def first_kernel(f_hbm, s_hbm, f_ref, low_ref, seg_ref, base_ref, pay_ref, f_in, s_in, f_buf, s_buf, sems):
    tiles, height = f_buf.shape[0], f_buf.shape[1]
    width = tiles * LANES
    seg = height // SUBS
    chunks = sems.shape[1]
    part = tiles // chunks
    copies = []
    for i in range(chunks):
        cols = pl.ds(i * part * LANES, part * LANES)
        copies.append(pltpu.make_async_copy(f_hbm.at[:, cols], f_in.at[:, cols], sems.at[0, i]))
        copies.append(pltpu.make_async_copy(s_hbm.at[:, cols], s_in.at[:, cols], sems.at[1, i]))
    for copy in copies:
        copy.start()
    sub = sub_index()
    for t in range(tiles):
        if t % part == 0:
            copies[2 * (t // part)].wait()
            copies[2 * (t // part) + 1].wait()
        cols = pl.ds(t * LANES, LANES)
        f_buf[t] = f_in[:, cols]
        s_buf[t] = jnp.where(s_in[:, cols] == 1, 0.0, HUGE)
        f = [f_buf[t, pl.ds(r, SUBS, stride=seg), :] for r in range(seg)]
        g = [s_buf[t, pl.ds(r, SUBS, stride=seg), :] for r in range(seg)]
        low = segment_pass(f, g)
        total = functools.reduce(lambda a, b: a + b, f)
        down, up, enter_d, enter_u = column_exits(f, low, total, sub)
        before, after, full = prefix_totals(total, sub)
        for r in range(seg):
            f_ref[r, t] = f[r]
            low_ref[r, t] = low[r]
        seg_ref[0, t] = enter_d
        seg_ref[1, t] = enter_u
        base_ref[0, t] = before
        base_ref[1, t] = after
        a, b = where_dense(t, width)
        pay_ref[0, pl.ds(a, 1), b] = down[SUBS - 1 : SUBS, :]
        pay_ref[1, pl.ds(a, 1), b] = up[0:1, :]
        pay_ref[2, pl.ds(a, 1), b] = full


def partner(mine, step, radix):
    return mine ^ step if radix & (radix - 1) == 0 else (mine + step) % radix


def sender(mine, step, radix):
    return mine ^ step if radix & (radix - 1) == 0 else (mine - step + radix) % radix


def join_kernel(stride, radix, trimmed, fresh, follow, *refs):
    refs = list(refs)
    own = refs.pop(0)
    pays = [refs.pop(0) for k in range(1, radix)]
    known = None if fresh else refs.pop(0)
    held = refs.pop(0) if stride > 1 else None
    tops = refs.pop()
    state = refs.pop(0)
    block = refs.pop(0) if follow else None
    totals = refs.pop(0) if fresh else known
    place = lax.axis_index("rows")
    mine = (place // stride) % radix
    tops[0, mine] = own[0]
    tops[1, mine] = own[1]
    if fresh:
        totals[mine] = own[2]
    for k in range(1, radix):
        m = sender(mine, k, radix)
        tops[0, m] = pays[k - 1][0]
        tops[1, m] = pays[k - 1][0 if trimmed else 1]
        if fresh:
            totals[m] = pays[k - 1][1 if trimmed else 2]
    shape = tops.shape[2:]
    exits = []
    for way in range(2):
        enter = run = jnp.full(shape, HUGE, jnp.float32)
        base = jnp.zeros(shape, jnp.float32)
        for m in range(radix) if way == 0 else range(radix - 1, -1, -1):
            enter = jnp.where(mine == m, run, enter)
            run = jnp.minimum(tops[way, m], run + totals[m])
            base = base + jnp.where(mine > m if way == 0 else mine < m, totals[m], 0.0)
        exits.append(run)
        if held is not None:
            enter = jnp.minimum(held[way], enter + held[2 + way])
            base = base + held[2 + way]
        state[way] = enter
        if follow:
            state[2 + way] = base
    if follow:
        block[0], block[1] = exits
        total = totals[0]
        for m in range(1, radix):
            total = total + totals[m]
        if fresh:
            block[2] = total
        if follow[2]:
            upper = (place // follow[0]) % follow[1]
            for k in range(1, follow[1]):
                pay = refs[k - 1]
                pay[0] = jnp.where(partner(upper, k, follow[1]) > upper, exits[0], exits[1])
                if fresh:
                    pay[1] = total


PIECES = 4


def spread(reach, low, axis):
    return (lane_roll if axis else sub_roll)(low, reach)


def ladder(total, index, step, count, axis):
    spans = []
    for sign in (1, -1):
        inside = index >= step if sign > 0 else index < step * (count - 1)
        span = jnp.where(inside, total, HUGE)
        reach = 1
        while reach < count:
            spans.append(span)
            span = span + spread(sign * step * reach, span, axis)
            reach *= 2
    return spans


def climb(low, spans, step, sign, axis):
    for k, span in enumerate(spans):
        low = jnp.minimum(low, spread(sign * (step << k), low, axis) + span)
    return low


def passed_totals(total, index, step, count, axis):
    found = []
    for sign in (1, -1):
        run = total
        reach = 1
        while reach < count:
            inside = index >= step * reach if sign > 0 else index < step * (count - reach)
            run = run + jnp.where(inside, spread(sign * step * reach, run, axis), 0.0)
            reach *= 2
        inside = index >= step if sign > 0 else index < step * (count - 1)
        found.append(jnp.where(inside, spread(sign * step, run, axis), 0.0))
    return found


def turn(stack, sheet, groups):
    for c in range(groups):
        sheet[c * LANES : (c + 1) * LANES, :] = stack[c].T


def turn_back(sheet, stack, groups):
    for c in range(groups):
        stack[c] = sheet[c * LANES : (c + 1) * LANES, :].T


def rows_of(r, t, groups, height):
    return t % groups, pl.ds((t // groups) * height + r * SUBS, SUBS)


def setup_kernel(f_ref, half_ref, sum_ref, aid_ref, stack, sheet):
    seg, tiles = f_ref.shape[0], f_ref.shape[1]
    height, groups, length = seg * SUBS, stack.shape[0], half_ref.shape[0]
    quarters = tiles // groups
    for t in range(tiles):
        for r in range(seg):
            c, rows = rows_of(r, t, groups, height)
            stack[c, rows, :] = 0.5 * f_ref[r, t]
    turn(stack, sheet, groups)
    size = length // PIECES
    runs = [None] * PIECES
    for i in range(size):
        for k in range(PIECES):
            at = k * size + i
            half = sheet[pl.ds(at, SUBS, stride=length), :]
            half_ref[at] = half
            runs[k] = half if i == 0 else runs[k] + half
    total = 0.0
    for k in range(PIECES):
        sum_ref[k] = runs[k] + runs[k]
        total = total + sum_ref[k]
    sub, lane = sub_index(), lane_index()
    aids = ladder(total, sub, 1, SUBS, 0)
    passed = passed_totals(total, sub, 1, SUBS, 0)
    full = total
    reach = 1
    while reach < SUBS:
        full = full + sub_roll(full, reach)
        reach *= 2
    aids += ladder(full, lane, height, quarters, 1)
    aids += passed + passed_totals(full, lane, height, quarters, 1)
    for k, aid in enumerate(aids):
        aid_ref[k] = aid


def aid_places(quarters):
    up, across = SUBS.bit_length() - 1, quarters.bit_length() - 1
    base = 2 * (up + across)
    return (
        [list(range(0, up)), list(range(up, 2 * up))],
        [list(range(2 * up, 2 * up + across)), list(range(2 * up + across, base))],
        [base, base + 1],
        [base + 2, base + 3],
    )


def across_kernel(enter, f_ref, low_ref, seg_ref, base_ref, half_ref, sum_ref, aid_ref,
                  out_ref, exit_ref, edge_ref, pay_ref, stack, sheet):
    seg, tiles = f_ref.shape[0], f_ref.shape[1]
    width = tiles * LANES
    height, groups, length = seg * SUBS, stack.shape[0], half_ref.shape[0]
    quarters = tiles // groups
    for t in range(tiles):
        a, b = where_dense(t, width)
        e_down = jnp.broadcast_to(enter[0, pl.ds(a, 1), b], (SUBS, LANES))
        e_up = jnp.broadcast_to(enter[1, pl.ds(a, 1), b], (SUBS, LANES))
        top = jnp.minimum(seg_ref[0, t], e_down + base_ref[0, t])
        bottom = jnp.minimum(seg_ref[1, t], e_up + base_ref[1, t])
        f = [f_ref[r, t] for r in range(seg)]
        half = [0.5 * x for x in f]
        c = [low_ref[r, t] for r in range(seg)]
        for r in range(seg):
            c[r] = jnp.minimum(c[r], top + half[r])
            top = top + f[r]
        for r in range(seg - 1, -1, -1):
            c[r] = jnp.minimum(c[r], bottom + half[r])
            bottom = bottom + f[r]
            at, rows = rows_of(r, t, groups, height)
            stack[at, rows, :] = c[r]
    turn(stack, sheet, groups)
    size = length // PIECES
    low = [None] * PIECES
    last = [None] * PIECES
    for i in range(size):
        for k in range(PIECES):
            at = k * size + i
            value, half = sheet[pl.ds(at, SUBS, stride=length), :], half_ref[at]
            low[k] = value if i == 0 else jnp.minimum(value, low[k] + (last[k] + half))
            last[k] = half
            out_ref[at] = low[k]
    rights = [low[k] + last[k] for k in range(PIECES)]
    for i in range(size - 2, -1, -1):
        for k in range(PIECES):
            at = k * size + i
            half = half_ref[at]
            low[k] = jnp.minimum(out_ref[at], low[k] + (last[k] + half))
            last[k] = half
            out_ref[at] = low[k]
    lefts = [low[k] + last[k] for k in range(PIECES)]
    sub, lane = sub_index(), lane_index()
    up_at, across_at, unused, unused = aid_places(quarters)
    ends = []
    for way, exits in enumerate((rights, lefts)):
        sign = 1 - 2 * way
        run = None
        for k in range(PIECES)[::sign]:
            exit_ref[way, k] = exits[k]
            run = exits[k] if run is None else jnp.minimum(exits[k], run + sum_ref[k])
        run = climb(run, [aid_ref[k] for k in up_at[way]], 1, sign, 0)
        inside = sub >= 1 if way == 0 else sub < SUBS - 1
        edge_ref[way] = jnp.where(inside, sub_roll(run, sign), HUGE)
        run = jnp.broadcast_to(run[SUBS - 1 : SUBS, :] if way == 0 else run[0:1, :], (SUBS, LANES))
        run = climb(run, [aid_ref[k] for k in across_at[way]], height, sign, 1)
        first, final = lane < height, lane >= LANES - height
        edge_ref[2 + way] = jnp.where(first if way == 0 else final, HUGE, lane_roll(run, sign * height))
        end = jnp.where(final if way == 0 else first, run, HUGE)
        reach = height
        while reach < LANES:
            end = jnp.minimum(end, lane_roll(end, reach))
            reach *= 2
        ends.append(end)
    pay_ref[...] = jnp.where(sub == 0, ends[0], ends[1])


def finish_rows(got_ref, row_ref, exit_ref, edge_ref, half_ref, sum_ref, aid_ref, quarters, buffer, emit):
    length = half_ref.shape[0]
    size = length // PIECES
    side = lax.axis_index("cols")
    unused, unused, sub_at, lane_at = aid_places(quarters)
    entries = []
    for way in range(2):
        sign = 1 - 2 * way
        enter = jnp.broadcast_to(got_ref[way : way + 1, :], (SUBS, LANES))
        enter = jnp.where(side > 0 if way == 0 else side == 0, enter, HUGE)
        enter = jnp.minimum(edge_ref[2 + way], enter + aid_ref[lane_at[way]])
        enter = jnp.minimum(edge_ref[way], enter + aid_ref[sub_at[way]])
        runs = [None] * PIECES
        for k in range(PIECES)[::sign]:
            runs[k] = enter
            enter = jnp.minimum(exit_ref[way, k], enter + sum_ref[k])
        entries.append(runs)
    rights, lefts = entries
    for i in range(size):
        for k in range(PIECES):
            at = k * size + i
            half = half_ref[at]
            here = rights[k] + half
            buffer[at] = jnp.minimum(row_ref[at], here)
            rights[k] = here + half
    for i in range(size - 1, -1, -1):
        for k in range(PIECES):
            at = k * size + i
            half = half_ref[at]
            here = lefts[k] + half
            emit(at, jnp.minimum(buffer[at], here))
            lefts[k] = here + half


def down_kernel(got_ref, row_ref, exit_ref, edge_ref, half_ref, sum_ref, aid_ref, f_ref,
                prev_ref, low_ref, seg_ref, pay_ref, stack, sheet):
    seg, tiles = f_ref.shape[0], f_ref.shape[1]
    width = tiles * LANES
    height, groups, length = seg * SUBS, stack.shape[0], half_ref.shape[0]

    def emit(at, value):
        prev_ref[at] = value
        sheet[pl.ds(at, SUBS, stride=length), :] = value

    finish_rows(got_ref, row_ref, exit_ref, edge_ref, half_ref, sum_ref, aid_ref, tiles // groups, prev_ref, emit)
    turn_back(sheet, stack, groups)
    sub = sub_index()
    for t in range(tiles):
        f = [f_ref[r, t] for r in range(seg)]
        c = []
        for r in range(seg):
            at, rows = rows_of(r, t, groups, height)
            c.append(stack[at, rows, :])
        low = segment_pass(f, c)
        total = functools.reduce(lambda a, b: a + b, f)
        down, up, enter_d, enter_u = column_exits(f, low, total, sub)
        for r in range(seg):
            low_ref[r, t] = low[r]
        seg_ref[0, t] = enter_d
        seg_ref[1, t] = enter_u
        a, b = where_dense(t, width)
        pay_ref[0, pl.ds(a, 1), b] = down[SUBS - 1 : SUBS, :]
        pay_ref[1, pl.ds(a, 1), b] = up[0:1, :]


def last_kernel(quarters, got_ref, row_ref, exit_ref, edge_ref, half_ref, sum_ref, aid_ref, prev_ref,
                sheet_ref, pay_ref, buffer):
    length = half_ref.shape[0]
    worst = [jnp.zeros((SUBS, LANES), jnp.float32) for k in range(PIECES)]

    def emit(at, value):
        sheet_ref[pl.ds(at, SUBS, stride=length), :] = value
        k = at % PIECES
        worst[k] = jnp.maximum(worst[k], prev_ref[at] - value)

    finish_rows(got_ref, row_ref, exit_ref, edge_ref, half_ref, sum_ref, aid_ref, quarters, buffer, emit)
    top = jnp.max(functools.reduce(jnp.maximum, worst), axis=0, keepdims=True)
    for e in range(pay_ref.shape[0]):
        pay_ref[e] = top


def output_kernel(seg, sheet_ref, cost_hbm, one_hbm, two_ref, stack, half_sheet, quarter_sheet,
                  cost_buf, one_buf, sems, sems_one):
    groups, length = stack.shape[0], sheet_ref.shape[0] // SUBS
    height = seg * SUBS
    quarters = LANES // height
    copies = []
    for c in range(groups):
        stack[c] = sheet_ref[c * LANES : (c + 1) * LANES, :].T
        for q in range(quarters):
            t = q * groups + c
            for r in range(seg):
                unused, rows = rows_of(r, t, groups, height)
                cost_buf[t, pl.ds(r, SUBS, stride=seg), :] = stack[c, rows, :]
            cols = pl.ds(t * LANES, LANES)
            copies.append(pltpu.make_async_copy(cost_buf.at[t], cost_hbm.at[:, cols], sems.at[t]))
            copies[-1].start()
    for i in range(length // 2):
        half_sheet[pl.ds(i, SUBS, stride=length // 2), :] = jnp.minimum(
            sheet_ref[pl.ds(2 * i, SUBS, stride=length), :],
            sheet_ref[pl.ds(2 * i + 1, SUBS, stride=length), :],
        )
    for c in range(groups // 2):
        stack[c] = half_sheet[c * LANES : (c + 1) * LANES, :].T
        for q in range(quarters):
            t = q * (groups // 2) + c
            for r in range(seg // 2):
                unused, above = rows_of(2 * r, t, groups // 2, height)
                unused, below = rows_of(2 * r + 1, t, groups // 2, height)
                one_buf[t, pl.ds(r, SUBS, stride=seg // 2), :] = jnp.minimum(stack[c, above, :], stack[c, below, :])
            cols = pl.ds(t * LANES, LANES)
            copies.append(pltpu.make_async_copy(one_buf.at[t], one_hbm.at[:, cols], sems_one.at[t]))
            copies[-1].start()
    for i in range(length // 4):
        quarter_sheet[pl.ds(i, SUBS, stride=length // 4), :] = jnp.minimum(
            half_sheet[pl.ds(2 * i, SUBS, stride=length // 2), :],
            half_sheet[pl.ds(2 * i + 1, SUBS, stride=length // 2), :],
        )
    for c in range(groups // 4):
        stack[c] = quarter_sheet[c * LANES : (c + 1) * LANES, :].T
        for q in range(quarters):
            t = q * (groups // 4) + c
            for r in range(seg // 4):
                low = None
                for k in range(4):
                    unused, rows = rows_of(4 * r + k, t, groups // 4, height)
                    low = stack[c, rows, :] if low is None else jnp.minimum(low, stack[c, rows, :])
                two_ref[r * SUBS : (r + 1) * SUBS, t * LANES : (t + 1) * LANES] = low
    for copy in copies:
        copy.wait()


def change_kernel(got_ref, out_ref):
    worst = jnp.max(got_ref[...], axis=0)
    worst = jnp.max(worst, axis=1, keepdims=True)
    out_ref[...] = jnp.broadcast_to(worst, out_ref.shape)


def scratch(*shape, dtype=jnp.float32):
    return pltpu.VMEM(shape, dtype)


def digits(count):
    stride, rest, found = 1, count, []
    while rest > 1:
        radix = next((k for k in (4, 2) if rest % k == 0), rest)
        found.append((stride, radix))
        stride, rest = stride * radix, rest // radix
    return [(s, r, 0 < i == len(found) - 1) for i, (s, r) in enumerate(found)]


def exchange(pay, known, peers):
    fresh = known is None
    short = pay.shape[1:]
    kinds = digits(peers)
    own, sent, state, totals = pay, None, None, []
    for i, (stride, radix, trimmed) in enumerate(kinds):
        follow = kinds[i + 1] if i + 1 < len(kinds) else None
        pays = []
        for k in range(1, radix):
            pairs = []
            for at in range(peers):
                mine = (at // stride) % radix
                pairs.append((at, at + (partner(mine, k, radix) - mine) * stride))
            pays.append(lax.ppermute(sent[k - 1] if trimmed else own, "rows", pairs))
        outs = [f32(4 if follow else 2, *short)]
        if follow:
            outs.append(f32(2 + fresh, *short))
        if fresh:
            outs.append(f32(radix, *short))
        if follow and follow[2]:
            outs += [f32(1 + fresh, *short)] * (follow[1] - 1)
        args = [own, *pays] + ([] if fresh else [known[i]]) + ([state] if stride > 1 else [])
        outs = list(
            pl.pallas_call(
                functools.partial(join_kernel, stride, radix, trimmed, fresh, follow),
                out_shape=outs,
                in_specs=[VMEM] * len(args),
                out_specs=[VMEM] * len(outs),
                scratch_shapes=[scratch(2, radix, *short)],
                compiler_params=PARAMS,
                name="join",
            )(*args)
        )
        state = outs.pop(0)
        own = outs.pop(0) if follow else None
        totals.append(outs.pop(0) if fresh else None)
        sent = outs
    return state, totals if fresh else known


def shards(friction, sources):
    height, width = friction.shape
    tiles, seg = width // LANES, height // SUBS
    quarters = LANES // height
    groups = tiles // quarters
    length = groups * LANES // SUBS
    peers, sides = lax.axis_size("rows"), lax.axis_size("cols")
    short = width // SUBS
    block = f32(seg, tiles, SUBS, LANES)
    pair = f32(2, tiles, SUBS, LANES)
    line = f32(length, SUBS, LANES)
    exits, edges = f32(2, PIECES, SUBS, LANES), f32(4, SUBS, LANES)
    turned = [scratch(groups, LANES, LANES), scratch(groups * LANES, LANES)]
    swap = [(i, sides - 1 - i) for i in range(sides)]
    chunks = 4

    f, low, enters, base, pay = pl.pallas_call(
        first_kernel,
        out_shape=(block, block, pair, pair, f32(3, SUBS, short)),
        in_specs=[ANY, ANY],
        out_specs=[VMEM] * 5,
        scratch_shapes=[
            scratch(height, width),
            scratch(height, width, dtype=jnp.int32),
            scratch(tiles, height, LANES),
            scratch(tiles, height, LANES),
            pltpu.SemaphoreType.DMA((2, chunks)),
        ],
        compiler_params=FIRST_PARAMS,
        name="first",
    )(friction, sources)
    lines = pl.pallas_call(
        setup_kernel,
        out_shape=(
            line,
            f32(PIECES, SUBS, LANES),
            f32(aid_places(quarters)[3][1] + 1, SUBS, LANES),
        ),
        in_specs=[VMEM],
        out_specs=[VMEM] * 3,
        scratch_shapes=turned,
        compiler_params=PARAMS,
        cost_estimate=pl.CostEstimate(flops=64 * height * width, bytes_accessed=16 * height * width, transcendentals=0),
        name="setup",
    )(f)
    enter, passed = exchange(pay, None, peers)

    def across(enter, low, enters):
        return pl.pallas_call(
            across_kernel,
            out_shape=(line, exits, edges, f32(SUBS, LANES)),
            in_specs=[VMEM] * 8,
            out_specs=[VMEM] * 4,
            scratch_shapes=turned,
            compiler_params=PARAMS,
            name="across",
        )(enter, f, low, enters, base, *lines)

    *rows, side_pay = across(enter, low, enters)
    side_got = lax.ppermute(side_pay, "cols", swap)
    prev, low, enters, pay = pl.pallas_call(
        down_kernel,
        out_shape=(line, block, pair, f32(2, SUBS, short)),
        in_specs=[VMEM] * 8,
        out_specs=[VMEM] * 4,
        scratch_shapes=turned,
        compiler_params=PARAMS,
        name="down",
    )(side_got, *rows, *lines, f)
    enter, passed = exchange(pay, passed, peers)
    *rows, side_pay = across(enter, low, enters)
    side_got = lax.ppermute(side_pay, "cols", swap)
    sheet, pay = pl.pallas_call(
        functools.partial(last_kernel, quarters),
        out_shape=(f32(groups * LANES, LANES), f32(peers * sides, 1, LANES)),
        in_specs=[VMEM] * 8,
        out_specs=[VMEM] * 2,
        scratch_shapes=[scratch(length, SUBS, LANES)],
        compiler_params=PARAMS,
        name="last",
    )(side_got, *rows, *lines, prev)
    got = lax.all_to_all(pay, ("rows", "cols"), 0, 0)
    cost, one, two = pl.pallas_call(
        functools.partial(output_kernel, seg),
        out_shape=(
            f32(height, width),
            f32(height // 2, width // 2),
            f32(height // 4, width // 4),
        ),
        in_specs=[VMEM],
        out_specs=[ANY, ANY, VMEM],
        scratch_shapes=[
            scratch(groups, LANES, LANES),
            scratch(groups * LANES // 2, LANES),
            scratch(groups * LANES // 4, LANES),
            scratch(tiles, height, LANES),
            scratch(tiles // 2, height // 2, LANES),
            pltpu.SemaphoreType.DMA((tiles,)),
            pltpu.SemaphoreType.DMA((tiles // 2,)),
        ],
        compiler_params=PARAMS,
        cost_estimate=pl.CostEstimate(flops=16 * height * width, bytes_accessed=16 * height * width, transcendentals=0),
        name="output",
    )(sheet)
    change = pl.pallas_call(
        change_kernel,
        out_shape=f32(1, LANES),
        in_specs=[VMEM],
        out_specs=VMEM,
        compiler_params=PARAMS,
        name="change",
    )(got)
    return cost, one, two, change[0, :1]


def solution(mesh):
    placed = (P("rows", "cols"), P("rows", "cols"))
    return jax.shard_map(
        shards,
        mesh=mesh,
        in_specs=placed,
        out_specs=(P("rows", "cols"), P("rows", "cols"), P("rows", "cols"), P()),
        check_vma=False,
    )
```
